32 devices in a mesh: depth: 4 (over z), row: 4 (over y, x), col: 2 (over core).
Axes of the slice: x: 2, y: 2, z: 4, core: 2. Of those that a mesh axis runs over, the one named last changes fastest.
Arguments:
- density: bfloat16 [32, 512, 512], P('depth', 'row', 'col'), may hold values from 0.009338379 to 0.1875
- emission: bfloat16 [3, 32, 512, 512], P(None, 'depth', 'row', 'col'), may hold values from 0.19921875 to 5
- offsets: int32 [3, 2, 4, 4, 4], P(None, None, 'depth', 'row', 'col'), may hold values from -8 to 8
- view_order: int32 [3, 4], P(None, 'row'), may hold values from 0 to 1
Outputs:
- image: float32 [3, 4, 128, 4, 512], P(None, None, 'row', 'depth', 'col')
The draws below stay inside these ranges and needn't reach their ends.
Inputs may be any that keep to these rules, and one draw needn't show every extreme that they name: `offsets`: displacement in cells of each brick's footprint from its home position in each view. `view_order`: 1 reverses the rays' direction along depth in that view and band of brick rows.
All inputs are finite; a program needn't handle non-finite values.
Results may differ from the reference program's by a relative error of at most 0.00052.
Values sent between devices are 32-bit elements; how exact they have to be, the bound alone decides.
No kernel may reach another device: no remote copies, remote signals or barrier semaphores. Data moves between devices by JAX's collectives and lax.ppermute only.
A program may use at most 128 MiB of HBM per device.

```python
import math
import jax
import jax.numpy as jnp
from jax import lax

BL = 128
MARGIN = 16
JIT = 8
BZ = 8
VIEWS = 3
TILE = 160
SLABS = 4
BROWS = 4
BCOLS = 4
ZCELLS = 32
YCELLS = 512
XCELLS = 512


def place_ends(values, key, least, high):
    shape = values.shape
    spot = [jax.random.randint(jax.random.fold_in(key, axis), (), 0, shape[axis]) for axis in range(len(shape))]
    values = values.at[tuple(spot)].set(least)
    longest = shape.index(max(shape))
    spot[longest] = (spot[longest] + 1) % shape[longest]
    return values.at[tuple(spot)].set(high)


def block_scale(stream_key, shape, shards, smallest, largest):
    gain = 1.0
    for axis_at, parts in shards:
        heights = jax.random.uniform(jax.random.fold_in(jax.random.fold_in(stream_key, 6), axis_at), (parts,), jnp.float32, smallest / len(shards), largest / len(shards))
        gain = gain * jnp.repeat(jnp.exp(heights), shape[axis_at] // parts).reshape((-1,) + (1,) * (len(shape) - 1 - axis_at))
    return gain


def setup_inputs(seed: int = 0) -> dict:
    splits = jax.random.split(jax.random.key(seed), 5)
    return {
        "density": jnp.clip(jnp.exp(math.log(0.1875) - 2.9996462 * jax.random.uniform(splits[0], (ZCELLS, YCELLS, XCELLS), jnp.float32) ** block_scale(splits[0], (ZCELLS, YCELLS, XCELLS), ((0, 4), (1, 4), (2, 2)), -0.2, 0.2)), 0.009338379, 0.1875).astype(jnp.bfloat16),
        "emission": jnp.clip(jnp.exp(math.log(5.0) - 3.2227897 * jax.random.uniform(splits[1], (3, ZCELLS, YCELLS, XCELLS), jnp.float32) ** block_scale(splits[1], (3, ZCELLS, YCELLS, XCELLS), ((1, 4), (2, 4), (3, 2)), -0.2, 0.2)), 0.19921875, 5.0).astype(jnp.bfloat16),
        "offsets": place_ends(jax.random.randint(splits[2], (VIEWS, 2, SLABS, BROWS, BCOLS), 0 - JIT, JIT + 1), jax.random.fold_in(splits[2], 1), 0 - JIT, JIT).astype(jnp.int32),
        "view_order": place_ends(jax.random.randint(splits[3], (VIEWS, BROWS), 0, 2), jax.random.fold_in(splits[3], 1), 0, 1).astype(jnp.int32),
    }


SHEAR_ROWS = (0.75, -0.5, 0.25)
SHEAR_COLS = (-0.25, 0.625, -0.875)


def bilinear(shear_rate, slices, length, margin):
    tile_width = length + 2 * margin
    slice_pos = jnp.arange(slices, dtype=jnp.float32)
    slice_shift = shear_rate * (margin - 2) * (2.0 * slice_pos - (slices - 1)) / slices
    target = jnp.arange(tile_width, dtype=jnp.float32)
    source = jnp.arange(length, dtype=jnp.float32)
    distance = target[None, :, None] - margin - slice_shift[:, None, None] - source[None, None, :]
    return jnp.maximum(0.0, 1.0 - jnp.abs(distance)).astype(jnp.bfloat16)


def integrate(footprint, backward):
    extinction = footprint[0]
    running = jnp.cumsum(extinction, axis=-3)
    total_depth = jnp.sum(extinction, axis=-3)
    prefix_depth = jnp.where(backward, total_depth[..., None, :, :] - running, running - extinction)
    weight = (1.0 - jnp.exp(-extinction)) * jnp.exp(-prefix_depth)
    colors = jnp.sum(footprint[1:] * weight, axis=-3)
    return jnp.concatenate([colors, total_depth[None]], 0)


def pad_along(source_array, lead_count, trail_count, axis_pos):
    widths = [(0, 0)] * source_array.ndim
    widths[axis_pos] = (lead_count, trail_count)
    return jnp.pad(source_array, widths)


def wrap_fold(canvas, rim_width, cell_count, axis_pos):
    interior = lax.slice_in_dim(canvas, rim_width, rim_width + cell_count, axis=axis_pos)
    head_rim = lax.slice_in_dim(canvas, 0, rim_width, axis=axis_pos)
    tail_rim = lax.slice_in_dim(canvas, rim_width + cell_count, cell_count + 2 * rim_width, axis=axis_pos)
    return interior + pad_along(head_rim, cell_count - rim_width, 0, axis_pos) + pad_along(tail_rim, 0, cell_count - rim_width, axis_pos)


def composite(slab_images, backward):
    depth_parts = slab_images[:, 3]
    running = jnp.cumsum(depth_parts, axis=0)
    depth_sum = running[-1]
    prefix_depth = jnp.where(backward, depth_sum[None] - running, running - depth_parts)
    colors = jnp.sum(slab_images[:, :3] * jnp.exp(-prefix_depth)[:, None], axis=0)
    return jnp.concatenate([colors, jnp.exp(-depth_sum)[None]], 0)


def reference(density, emission, offsets, view_order):
    fields = jnp.concatenate([density[None], emission], 0)
    rim_width = MARGIN + JIT
    per_view = []
    for view_index in range(VIEWS):
        row_weights = bilinear(SHEAR_ROWS[view_index], BZ, BL, MARGIN).astype(jnp.float32)
        col_weights = bilinear(SHEAR_COLS[view_index], BZ, BL, MARGIN).astype(jnp.float32)
        band_orders = view_order[view_index]

        def deposit(canvas, brick_flat):
            slab_index = brick_flat // (BROWS * BCOLS)
            remainder = brick_flat % (BROWS * BCOLS)
            brick_row = remainder // BCOLS
            brick_col = remainder % BCOLS
            brick_cells = lax.dynamic_slice(
                fields,
                (jnp.int32(0), (slab_index * BZ).astype(jnp.int32), (brick_row * BL).astype(jnp.int32), (brick_col * BL).astype(jnp.int32)),
                (4, BZ, BL, BL))
            resampled = jnp.einsum("fzyx,zux->fzyu", brick_cells.astype(jnp.float32), col_weights).astype(jnp.bfloat16)
            footprint = jnp.einsum("zty,fzyu->fztu", row_weights, resampled.astype(jnp.float32))
            shaded = integrate(footprint, band_orders[brick_row] == 1)
            top_row = (brick_row * BL + offsets[view_index, 0, slab_index, brick_row, brick_col] + JIT).astype(jnp.int32)
            left_col = (brick_col * BL + offsets[view_index, 1, slab_index, brick_row, brick_col] + JIT).astype(jnp.int32)
            corner = (slab_index.astype(jnp.int32), jnp.int32(0), top_row, left_col)
            current = lax.dynamic_slice(canvas, corner, (1, 4, TILE, TILE))
            return lax.dynamic_update_slice(canvas, current + shaded[None], corner), None

        canvas = jnp.zeros((SLABS, 4, YCELLS + 2 * rim_width, XCELLS + 2 * rim_width), jnp.float32)
        canvas, unused = lax.scan(deposit, canvas, jnp.arange(SLABS * BROWS * BCOLS, dtype=jnp.int32))
        slab_images = wrap_fold(wrap_fold(canvas, rim_width, YCELLS, 2), rim_width, XCELLS, 3)
        row_backward = (jnp.repeat(band_orders, BL) == 1)[:, None]
        per_view.append(composite(slab_images, row_backward))
    image_all = jnp.stack(per_view)
    return image_all.reshape(VIEWS, 4, YCELLS // SLABS, SLABS, XCELLS)
```

```python
import functools
import math
import jax
import jax.numpy as jnp
from jax import lax
from jax.experimental import pallas as pl
from jax.experimental.pallas import tpu as pltpu
from jax.sharding import PartitionSpec as P

MARGIN = 16
JIT = 8
VIEWS = 3

SHEAR_ROWS = (0.75, -0.5, 0.25)
SHEAR_COLS = (-0.25, 0.625, -0.875)

TILE = 8
BF = jnp.bfloat16
F32 = jnp.float32
SMEM = pl.BlockSpec(memory_space=pltpu.SMEM)
VMEM = pl.BlockSpec(memory_space=pltpu.VMEM)
ANY = pl.BlockSpec(memory_space=pl.ANY)


def shared_spill(view, slices, phases):
    reach = abs(SHEAR_ROWS[view]) * (MARGIN - 2) * (slices - 1) / slices + JIT + 1
    need = -(-(math.ceil(reach) - 1) // phases)
    assert need <= TILE and phases & (phases - 1) == 0
    return 2 * need <= TILE


def canvas_rows(view, slices, phases, length):
    return length + (1 if shared_spill(view, slices, phases) else 2) * TILE * phases


def render_kernel(view, phases, offs, order, dens, emis, home, rim, dbuf, ebuf, drow, dcol, hs, rs, sem):
    slices, length, columns = dens.shape
    bricks = columns // length
    half = length // 2
    quota = length // phases
    back = order[view, 0] == 1

    def slice_at(k):
        return jnp.where(back, slices - 1 - k, k)

    def copies(z):
        return (
            pltpu.make_async_copy(dens.at[z], dbuf.at[z], sem.at[0, z]),
            pltpu.make_async_copy(emis.at[:, z], ebuf.at[:, z], sem.at[1, z]),
        )

    for k in range(slices):
        for copy in copies(slice_at(k)):
            copy.start()

    def row_table(count, place):
        shape = (phases, count, length)
        phase = lax.broadcasted_iota(jnp.int32, shape, 0)
        spot = lax.broadcasted_iota(jnp.int32, shape, 1)
        source = lax.broadcasted_iota(jnp.int32, shape, 2)
        return (place(spot) * phases + phase - source).astype(F32).reshape(phases * count, length)

    spill = TILE * phases
    drow[0:length] = row_table(quota, lambda spot: spot)
    if drow.shape[0] == length + spill:
        drow[length:] = row_table(
            TILE, lambda spot: jnp.where(spot < TILE // 2, spot + quota, spot - TILE)
        )
    else:
        drow[length : length + spill] = row_table(TILE, lambda spot: spot - TILE)
        drow[length + spill :] = row_table(TILE, lambda spot: spot + quota)
    lane = lax.broadcasted_iota(jnp.int32, (length, length), 1)
    source = lax.broadcasted_iota(jnp.int32, (length, length), 0)
    dcol[0] = (lane - source).astype(F32)
    dcol[1] = (jnp.where(lane < half, lane + length, lane - length) - source).astype(F32)
    dcol[2] = (jnp.where(lane < half, lane - half, lane + half) - source).astype(F32)
    for ref in (home, rim):
        ref[0:3] = jnp.zeros((3,) + ref.shape[1:], F32)
        ref[3] = jnp.ones(ref.shape[1:], F32)

    def step(k, carry):
        z = slice_at(k)
        for copy in copies(z):
            copy.wait()
        spot = (2 * z - (slices - 1)).astype(F32)
        row_shift = spot * (SHEAR_ROWS[view] * (MARGIN - 2) / slices)
        col_shift = spot * (SHEAR_COLS[view] * (MARGIN - 2) / slices)
        row_weights = []
        for b in range(bricks):
            part = slice(b * length, (b + 1) * length)
            left = offs[view, 1, 0, 0, b].astype(F32) + col_shift
            top = offs[view, 0, 0, 0, b].astype(F32) + row_shift
            distance = jnp.concatenate([dcol[0], dcol[1 + b]], 1) - left
            col_weights = jnp.maximum(0.0, 1.0 - jnp.abs(distance)).astype(BF)
            cells = [dbuf[z, :, part]] + [ebuf[c, z, :, part] for c in range(3)]
            for f in range(4):
                resampled = jnp.dot(cells[f], col_weights, preferred_element_type=F32).astype(BF)
                field = slice(f * length, (f + 1) * length)
                hs[b, :, field] = resampled[:, :length]
                rs[part, field] = resampled[:, length:]
            row_weights.append(jnp.maximum(0.0, 1.0 - jnp.abs(drow[...] - top)).astype(BF))

        def shade(footprint, ref, part):
            through = ref[3, :, part]
            passed = through * jnp.exp(-footprint[:, :length])
            weight = through - passed
            ref[3, :, part] = passed
            for c in range(3):
                color = footprint[:, (c + 1) * length : (c + 2) * length]
                ref[c, :, part] = ref[c, :, part] + color * weight

        for b in range(bricks):
            shade(
                jnp.dot(row_weights[b], hs[b], preferred_element_type=F32),
                home,
                slice(b * length, (b + 1) * length),
            )
        both = jnp.concatenate(row_weights, 1)
        shade(jnp.dot(both, rs[...], preferred_element_type=F32), rim, slice(0, length))
        return carry

    lax.fori_loop(0, slices, step, 0)


def render(view, phases, offsets, orders, density, emission):
    slices, length, columns = density.shape
    rows = canvas_rows(view, slices, phases, length)
    bricks = columns // length
    assert bricks == 2 and length == 128
    return pl.pallas_call(
        functools.partial(render_kernel, view, phases),
        out_shape=(
            jax.ShapeDtypeStruct((4, rows, columns), F32),
            jax.ShapeDtypeStruct((4, rows, length), F32),
        ),
        in_specs=[SMEM, SMEM, ANY, ANY],
        out_specs=(VMEM, VMEM),
        scratch_shapes=[
            pltpu.VMEM(density.shape, BF),
            pltpu.VMEM(emission.shape, BF),
            pltpu.VMEM((rows, length), F32),
            pltpu.VMEM((3, length, length), F32),
            pltpu.VMEM((bricks, length, 4 * length), BF),
            pltpu.VMEM((bricks * length, 4 * length), BF),
            pltpu.SemaphoreType.DMA((2, slices)),
        ],
        name=f"render{view}",
    )(offsets, orders, density, emission)


def joined(channel, one, other):
    return one * other if channel == 3 else one + other


def fold_kernel(shared, phases, home, rim, low, high, *outs):
    rows, columns = home.shape[1:]
    lanes = columns // 2
    half, quarter = lanes // 2, lanes // 4
    quota = (rows - (1 if shared else 2) * TILE * phases) // phases
    length = quota * phases
    inner, (edge, up, down) = outs[:-3], outs[-3:]
    me = lax.axis_index("depth")

    def folded(c, start, count):
        part = pl.ds(start, count)
        lane = lax.broadcasted_iota(jnp.int32, (count, lanes), 1)
        neutral = 1.0 if c == 3 else 0.0
        own = rim[c, part]
        first = jnp.where(lane < half, own, low[c, part])
        first = jnp.where((lane >= quarter) & (lane < lanes - quarter), first, neutral)
        second = jnp.where(lane < half, own, high[c, part])
        second = jnp.where((lane < quarter) | (lane >= lanes - quarter), second, neutral)
        return (
            joined(c, home[c, part, 0:lanes], pltpu.roll(first, half, 1)),
            joined(c, home[c, part, lanes:columns], second),
        )

    for c in range(4):
        for p in range(phases):
            for side, start in enumerate((0, quota - TILE)):
                spot = slice(side * TILE, (side + 1) * TILE)
                one, other = folded(c, p * quota + start, TILE)
                edge[c, p, spot, 0:lanes] = one
                edge[c, p, spot, lanes:columns] = other
        for k, out in enumerate(inner):
            start = pl.multiple_of((me ^ k) * quota + TILE, TILE)
            one, other = folded(c, start, quota - 2 * TILE)
            out[c, :, 0:lanes] = one
            out[c, :, lanes:columns] = other
        if shared:
            sub = lax.broadcasted_iota(jnp.int32, (TILE, lanes), 0)
            for j in range(phases // 2):
                one = folded(c, length + 2 * j * TILE, TILE)
                other = folded(c, length + (2 * j + 1) * TILE, TILE)
                for n in range(2):
                    turned = pltpu.roll(other[n], TILE // 2, 0)
                    part = slice(n * lanes, (n + 1) * lanes)
                    up[c, j, :, part] = jnp.where(sub < TILE // 2, turned, one[n])
                    down[c, j, :, part] = jnp.where(sub < TILE // 2, one[n], turned)
        else:
            for p in range(phases):
                for n, out in enumerate((up, down)):
                    one, other = folded(c, length + (n * phases + p) * TILE, TILE)
                    out[c, p, :, 0:lanes] = one
                    out[c, p, :, lanes:columns] = other


def fold(view, slices, length, phases, home, rim, low, high):
    columns = home.shape[2]
    shared = shared_spill(view, slices, phases)
    quota = length // phases
    packs = phases // 2 if shared else phases
    shapes = [(4, quota - 2 * TILE, columns)] * (phases if quota > 2 * TILE else 0)
    shapes += [(4, phases, 2 * TILE, columns)] + [(4, packs, TILE, columns)] * 2
    outs = pl.pallas_call(
        functools.partial(fold_kernel, shared, phases),
        out_shape=tuple(jax.ShapeDtypeStruct(shape, F32) for shape in shapes),
        in_specs=[VMEM] * 4,
        out_specs=(VMEM,) * len(shapes),
        name=f"fold{view}",
    )(home, rim, low, high)
    return outs[:-3], *outs[-3:]


def edge_kernel(shared, phases, edge, above, below, *outs):
    me = lax.axis_index("depth")
    for k in range(phases):
        p = me ^ k
        for c in range(4):
            if shared:
                neutral = 1.0 if c == 3 else 0.0
                sub = lax.broadcasted_iota(jnp.int32, above.shape[2:], 0)
                odd = (p & 1) == 1
                top, bottom = above[c, p >> 1], below[c, p >> 1]
                top = jnp.where(odd, pltpu.roll(top, TILE // 2, 0), top)
                bottom = jnp.where(odd, pltpu.roll(bottom, TILE // 2, 0), bottom)
                top = jnp.where(sub < TILE // 2, top, neutral)
                bottom = jnp.where(sub < TILE // 2, neutral, bottom)
            else:
                top, bottom = above[c, p], below[c, p]
            outs[k][c, 0:TILE] = joined(c, edge[c, p, 0:TILE], top)
            outs[k][c, TILE:] = joined(c, edge[c, p, TILE:], bottom)


def finish_edges(view, shared, phases, edge, above, below):
    shape = jax.ShapeDtypeStruct((4, 2 * TILE, edge.shape[3]), F32)
    return pl.pallas_call(
        functools.partial(edge_kernel, shared, phases),
        out_shape=(shape,) * phases,
        in_specs=[VMEM] * 3,
        out_specs=(VMEM,) * phases,
        name=f"edge{view}",
    )(edge, above, below)


def over_kernel(view, phases, layers, order, *refs):
    edges, inner = refs[:phases], refs[phases : layers]
    out, stage, sem = refs[-3:]
    backward = order[view, 0] == 1
    me = lax.axis_index("depth")
    count = stage.shape[1]

    def composed(parts):
        bit = 0
        while len(parts) > 1:
            first = jnp.logical_xor((me >> bit & 1) == 0, backward)
            paired = []
            for one, other in zip(parts[0::2], parts[1::2]):
                front = [jnp.where(first, a, b) for a, b in zip(one, other)]
                rear = [jnp.where(first, b, a) for a, b in zip(one, other)]
                paired.append([f + front[3] * r for f, r in zip(front[:3], rear[:3])] + [front[3] * rear[3]])
            parts = paired
            bit += 1
        return parts[0]

    for start, refset, at, size in (
        (0, edges, 0, TILE),
        (TILE, inner, 0, count - 2 * TILE),
        (count - TILE, edges, TILE, TILE),
    ):
        if size == 0:
            continue
        pixels = composed([[ref[c, at : at + size] for c in range(4)] for ref in refset])
        for c in range(4):
            stage[c, start : start + size] = pixels[c]
    copy = pltpu.make_async_copy(stage, out.at[view], sem)
    copy.start()
    copy.wait()


def composite(view, phases, orders, inner, edges, image):
    columns = edges[0].shape[2]
    quota = (inner[0].shape[1] if inner else 0) + 2 * TILE
    operands = [orders, *edges, *inner]
    specs = [SMEM] + [VMEM] * (phases + len(inner))
    aliases = {}
    if image is not None:
        operands.append(image)
        specs.append(ANY)
        aliases = {len(operands) - 1: 0}
    return pl.pallas_call(
        functools.partial(over_kernel, view, phases, phases + len(inner)),
        out_shape=jax.ShapeDtypeStruct((VIEWS, 4, quota, columns), F32),
        in_specs=specs,
        out_specs=ANY,
        scratch_shapes=[pltpu.VMEM((4, quota, columns), F32), pltpu.SemaphoreType.DMA],
        input_output_aliases=aliases,
        name=f"over{view}",
    )(*operands)


def shifted(block, axis, step):
    count = lax.axis_size(axis)
    return lax.ppermute(block, axis, [(i, (i + step) % count) for i in range(count)])


def spread(blocks):
    count = lax.axis_size("depth")
    return [
        block if k == 0 else lax.ppermute(block, "depth", [(i, i ^ k) for i in range(count)])
        for k, block in enumerate(blocks)
    ]


def local(density, emission, offsets, view_order):
    slices, length = density.shape[:2]
    phases = lax.axis_size("depth")
    image = None
    for view in range(VIEWS):
        home, rim = render(view, phases, offsets, view_order, density, emission)
        low = shifted(rim, "col", 1)
        high = low if lax.axis_size("col") == 2 else shifted(rim, "col", -1)
        inner, edge, up, down = fold(view, slices, length, phases, home, rim, low, high)
        inner = spread(inner)
        above = shifted(down, "row", 1)
        below = shifted(up, "row", -1)
        edges = spread(
            finish_edges(view, shared_spill(view, slices, phases), phases, edge, above, below)
        )
        image = composite(view, phases, view_order, inner, edges, image)
    return image[:, :, :, None, :]


def solution(mesh):
    return jax.shard_map(
        local,
        mesh=mesh,
        in_specs=(
            P("depth", "row", "col"),
            P(None, "depth", "row", "col"),
            P(None, None, "depth", "row", "col"),
            P(None, "row"),
        ),
        out_specs=P(None, None, "row", "depth", "col"),
        check_vma=False,
    )
```

```python
import functools
import math
import jax
import jax.numpy as jnp
from jax import lax
from jax.experimental import pallas as pl
from jax.experimental.pallas import tpu as pltpu
from jax.sharding import PartitionSpec as P

MARGIN = 16
JIT = 8
VIEWS = 3

SHEAR_ROWS = (0.75, -0.5, 0.25)
SHEAR_COLS = (-0.25, 0.625, -0.875)

TILE = 8
GRID = 32
BF = jnp.bfloat16
F32 = jnp.float32
SMEM = pl.BlockSpec(memory_space=pltpu.SMEM)
VMEM = pl.BlockSpec(memory_space=pltpu.VMEM)
ANY = pl.BlockSpec(memory_space=pl.ANY)


def near(shape):
    return pltpu.VMEM(shape, F32)


def held(*arrays):
    return [pltpu.with_memory_space_constraint(array, pltpu.VMEM) for array in arrays]


def shared_spill(view, slices, phases):
    reach = abs(SHEAR_ROWS[view]) * (MARGIN - 2) * (slices - 1) / slices + JIT + 1
    need = -(-(math.ceil(reach) - 1) // phases)
    assert need <= TILE and phases & (phases - 1) == 0
    return 2 * need <= TILE


def canvas_rows(view, slices, phases, length):
    return length + (1 if shared_spill(view, slices, phases) else 2) * TILE * phases


def render_kernel(view, phases, offs, order, dens, emis, home, rim, dbuf, ebuf, drow, dcol, hs, rs, sem):
    slices, length, columns = dens.shape
    bricks = columns // length
    half = length // 2
    quota = length // phases
    back = order[0, view] == 1

    def slice_at(k):
        return jnp.where(back, slices - 1 - k, k)

    def copies(z):
        return (
            pltpu.make_async_copy(dens.at[z], dbuf.at[z], sem.at[0, z]),
            pltpu.make_async_copy(emis.at[:, z], ebuf.at[:, z], sem.at[1, z]),
        )

    for k in range(slices):
        for copy in copies(slice_at(k)):
            copy.start()

    def row_table(count, place):
        shape = (phases, count, length)
        phase = lax.broadcasted_iota(jnp.int32, shape, 0)
        spot = lax.broadcasted_iota(jnp.int32, shape, 1)
        source = lax.broadcasted_iota(jnp.int32, shape, 2)
        table = place(spot) * phases + phase - source
        return table.astype(F32).reshape(phases * count, length).astype(BF)

    spill = TILE * phases
    drow[0:length] = row_table(quota, lambda spot: spot)
    if drow.shape[0] == length + spill:
        drow[length:] = row_table(
            TILE, lambda spot: jnp.where(spot < TILE // 2, spot + quota, spot - TILE)
        )
    else:
        drow[length : length + spill] = row_table(TILE, lambda spot: spot - TILE)
        drow[length + spill :] = row_table(TILE, lambda spot: spot + quota)
    lane = lax.broadcasted_iota(jnp.int32, (length, length), 1)
    source = lax.broadcasted_iota(jnp.int32, (length, length), 0)
    dcol[0] = (lane - source).astype(F32).astype(BF)
    dcol[1] = (jnp.where(lane < half, lane + length, lane - length) - source).astype(F32).astype(BF)
    dcol[2] = (jnp.where(lane < half, lane - half, lane + half) - source).astype(F32).astype(BF)
    for ref in (home, rim):
        ref[0:3] = jnp.zeros((3,) + ref.shape[1:], F32)
        ref[3] = jnp.ones(ref.shape[1:], F32)

    def bilinear(distance, offset, rate, z):
        grid_rate = rate * (MARGIN - 2) * GRID / slices
        assert grid_rate == int(grid_rate)
        shift = offset * GRID + (2 * z - (slices - 1)) * int(grid_rate)
        whole = shift >> (GRID.bit_length() - 1)
        rest = (shift & (GRID - 1)).astype(F32) * (1.0 / GRID)
        near = (distance - whole.astype(F32).astype(BF)) - rest.astype(BF)
        one = jnp.ones((), BF)
        return jnp.maximum(one - jnp.abs(near), jnp.zeros((), BF))

    def resample(k, slot):
        z = slice_at(k)
        for copy in copies(z):
            copy.wait()
        for b in range(bricks):
            part = slice(b * length, (b + 1) * length)
            distance = jnp.concatenate([dcol[0], dcol[1 + b]], 1)
            weights = bilinear(distance, offs[1, 0, 0, b, view], SHEAR_COLS[view], z)
            cells = jnp.concatenate([dbuf[z, :, part]] + [ebuf[c, z, :, part] for c in range(3)], 0)
            resampled = jnp.dot(cells, weights, preferred_element_type=F32).astype(BF)
            for f in range(4):
                field = slice(f * length, (f + 1) * length)
                hs[slot, b, :, field] = resampled[field, :length]
                rs[slot, part, field] = resampled[field, length:]

    def shade(footprint, ref, part):
        through = ref[3, :, part]
        passed = through * jnp.exp(-footprint[:, :length])
        weight = through - passed
        ref[3, :, part] = passed
        for c in range(3):
            color = footprint[:, (c + 1) * length : (c + 2) * length]
            ref[c, :, part] = ref[c, :, part] + color * weight

    def deposit(k, slot):
        z = slice_at(k)
        weights = [
            bilinear(drow[...], offs[0, 0, 0, b, view], SHEAR_ROWS[view], z) for b in range(bricks)
        ]
        for b in range(bricks):
            shade(
                jnp.dot(weights[b], hs[slot, b], preferred_element_type=F32),
                home,
                slice(b * length, (b + 1) * length),
            )
        both = jnp.concatenate(weights, 1)
        shade(jnp.dot(both, rs[slot], preferred_element_type=F32), rim, slice(0, length))

    resample(0, 0)

    def step(pair, carry):
        k = 2 * pair
        resample(k + 1, 1)
        deposit(k, 0)
        resample(k + 2, 0)
        deposit(k + 1, 1)
        return carry

    assert slices % 2 == 0
    lax.fori_loop(0, slices // 2 - 1, step, 0)
    resample(slices - 1, 1)
    deposit(slices - 2, 0)
    deposit(slices - 1, 1)


def render(view, phases, offsets, orders, density, emission):
    slices, length, columns = density.shape
    rows = canvas_rows(view, slices, phases, length)
    bricks = columns // length
    assert bricks == 2 and length == 128
    return pl.pallas_call(
        functools.partial(render_kernel, view, phases),
        out_shape=(near((4, rows, columns)), near((4, rows, length))),
        in_specs=[SMEM, SMEM, ANY, ANY],
        out_specs=(VMEM, VMEM),
        scratch_shapes=[
            pltpu.VMEM(density.shape, BF),
            pltpu.VMEM(emission.shape, BF),
            pltpu.VMEM((rows, length), BF),
            pltpu.VMEM((3, length, length), BF),
            pltpu.VMEM((2, bricks, length, 4 * length), BF),
            pltpu.VMEM((2, bricks * length, 4 * length), BF),
            pltpu.SemaphoreType.DMA((2, slices)),
        ],
        compiler_params=pltpu.CompilerParams(vmem_limit_bytes=16 << 20),
        name=f"render{view}",
    )(offsets, orders, *(pltpu.with_memory_space_constraint(array, pltpu.HBM) for array in (density, emission)))


def joined(channel, one, other):
    return one * other if channel == 3 else one + other


def fold_kernel(shared, phases, home, rim, low, high, canvas, up, down):
    columns = home.shape[2]
    lanes = columns // 2
    half, quarter = lanes // 2, lanes // 4
    quota = canvas.shape[2]
    length = quota * phases

    def folded(c, start, count):
        part = pl.ds(start, count)
        lane = lax.broadcasted_iota(jnp.int32, (count, lanes), 1)
        neutral = 1.0 if c == 3 else 0.0
        own = rim[c, part]
        first = jnp.where(lane < half, own, low[c, part])
        first = jnp.where((lane >= quarter) & (lane < lanes - quarter), first, neutral)
        second = jnp.where(lane < half, own, high[c, part])
        second = jnp.where((lane < quarter) | (lane >= lanes - quarter), second, neutral)
        return (
            joined(c, home[c, part, 0:lanes], pltpu.roll(first, half, 1)),
            joined(c, home[c, part, lanes:columns], second),
        )

    for c in range(4):
        for p in range(phases):
            one, other = folded(c, p * quota, quota)
            canvas[c, p, :, 0:lanes] = one
            canvas[c, p, :, lanes:columns] = other
        if shared:
            sub = lax.broadcasted_iota(jnp.int32, (TILE, lanes), 0)
            for j in range(phases // 2):
                one = folded(c, length + 2 * j * TILE, TILE)
                other = folded(c, length + (2 * j + 1) * TILE, TILE)
                for n in range(2):
                    turned = pltpu.roll(other[n], TILE // 2, 0)
                    part = slice(n * lanes, (n + 1) * lanes)
                    up[c, j, :, part] = jnp.where(sub < TILE // 2, turned, one[n])
                    down[c, j, :, part] = jnp.where(sub < TILE // 2, one[n], turned)
        else:
            for p in range(phases):
                for n, out in enumerate((up, down)):
                    one, other = folded(c, length + (n * phases + p) * TILE, TILE)
                    out[c, p, :, 0:lanes] = one
                    out[c, p, :, lanes:columns] = other


def fold(view, slices, length, phases, home, rim, low, high):
    columns = home.shape[2]
    shared = shared_spill(view, slices, phases)
    packs = phases // 2 if shared else phases
    return pl.pallas_call(
        functools.partial(fold_kernel, shared, phases),
        out_shape=(
            near((4, phases, length // phases, columns)),
            near((4, packs, TILE, columns)),
            near((4, packs, TILE, columns)),
        ),
        in_specs=[VMEM] * 4,
        out_specs=(VMEM,) * 3,
        compiler_params=pltpu.CompilerParams(vmem_limit_bytes=4 << 20),
        name=f"fold{view}",
    )(*held(home, rim, low, high))


def finish_kernel(shared, canvas, above, below, kept, given):
    me = lax.axis_index("depth")
    bit = me & 1
    quota = canvas.shape[2]
    for n in range(kept.shape[1]):
        for out, odd in ((kept, bit), (given, 1 - bit)):
            p = 2 * n + odd
            for c in range(4):
                if shared:
                    neutral = 1.0 if c == 3 else 0.0
                    sub = lax.broadcasted_iota(jnp.int32, above.shape[2:], 0)
                    top, bottom = above[c, n], below[c, n]
                    top = jnp.where(odd == 1, pltpu.roll(top, TILE // 2, 0), top)
                    bottom = jnp.where(odd == 1, pltpu.roll(bottom, TILE // 2, 0), bottom)
                    top = jnp.where(sub < TILE // 2, top, neutral)
                    bottom = jnp.where(sub < TILE // 2, neutral, bottom)
                else:
                    top, bottom = above[c, p], below[c, p]
                out[c, n, 0:TILE] = joined(c, canvas[c, p, 0:TILE], top)
                if quota > 2 * TILE:
                    out[c, n, TILE : quota - TILE] = canvas[c, p, TILE : quota - TILE]
                out[c, n, quota - TILE :] = joined(c, canvas[c, p, quota - TILE :], bottom)


def finish(view, shared, canvas, above, below):
    channels, phases, quota, columns = canvas.shape
    return pl.pallas_call(
        functools.partial(finish_kernel, shared),
        out_shape=(near((channels, phases // 2, quota, columns)),) * 2,
        in_specs=[VMEM] * 3,
        out_specs=(VMEM,) * 2,
        compiler_params=pltpu.CompilerParams(vmem_limit_bytes=4 << 20),
        name=f"finish{view}",
    )(*held(canvas, above, below))


def over(own_first, own, other):
    front = [jnp.where(own_first, a, b) for a, b in zip(own, other)]
    rear = [jnp.where(own_first, b, a) for a, b in zip(own, other)]
    return [f + front[3] * r for f, r in zip(front[:3], rear[:3])] + [front[3] * rear[3]]


def own_first(view, level, order):
    me = lax.axis_index("depth")
    return jnp.logical_xor((me >> level & 1) == 0, order[0, view] == 1)


def merge_kernel(view, level, order, kept, received, next_kept, next_given):
    ahead = own_first(view, level, order)
    bit = lax.axis_index("depth") >> (level + 1) & 1
    for n in range(next_kept.shape[1]):
        for out, odd in ((next_kept, bit), (next_given, 1 - bit)):
            p = 2 * n + odd
            pixels = over(ahead, [kept[c, p] for c in range(4)], [received[c, p] for c in range(4)])
            for c in range(4):
                out[c, n] = pixels[c]


def merge(view, level, orders, kept, received):
    channels, phases, quota, columns = kept.shape
    return pl.pallas_call(
        functools.partial(merge_kernel, view, level),
        out_shape=(near((channels, phases // 2, quota, columns)),) * 2,
        in_specs=[SMEM] + [VMEM] * 2,
        out_specs=(VMEM,) * 2,
        compiler_params=pltpu.CompilerParams(vmem_limit_bytes=4 << 20),
        name=f"merge{view}_{level}",
    )(orders, *held(kept, received))


def emit_kernel(view, level, order, kept, received, *refs):
    out, stage, sem = refs[-3:]
    ahead = own_first(view, level, order)
    quota, columns = kept.shape[2:]
    lanes = stage.shape[2]
    pieces = columns // lanes
    pixels = over(ahead, [kept[c, 0] for c in range(4)], [received[c, 0] for c in range(4)])
    for c in range(4):
        for n in range(pieces):
            stage[c, pl.ds(n, quota, stride=pieces), :] = pixels[c][:, n * lanes : (n + 1) * lanes]
    copy = pltpu.make_async_copy(stage, out.at[view], sem)
    copy.start()
    copy.wait()


def emit(view, level, orders, kept, received, image):
    channels, _, quota, columns = kept.shape
    shape = (channels, quota * columns // 128, 128)
    operands = [orders, *held(kept, received)]
    specs = [SMEM, VMEM, VMEM]
    aliases = {}
    if image is not None:
        operands.append(image)
        specs.append(ANY)
        aliases = {3: 0}
    return pl.pallas_call(
        functools.partial(emit_kernel, view, level),
        out_shape=jax.ShapeDtypeStruct((VIEWS,) + shape, F32),
        in_specs=specs,
        out_specs=ANY,
        scratch_shapes=[pltpu.VMEM(shape, F32), pltpu.SemaphoreType.DMA],
        input_output_aliases=aliases,
        compiler_params=pltpu.CompilerParams(vmem_limit_bytes=4 << 20),
        name=f"emit{view}",
    )(*operands)


def shifted(block, axis, step):
    count = lax.axis_size(axis)
    return lax.ppermute(block, axis, [(i, (i + step) % count) for i in range(count)])


def swapped(block, level):
    count = lax.axis_size("depth")
    return lax.ppermute(block, "depth", [(i, i ^ 1 << level) for i in range(count)])


def local(density, emission, offsets, view_order):
    slices, length, columns = density.shape
    phases = lax.axis_size("depth")
    levels = phases.bit_length() - 1
    offsets = offsets.transpose(1, 2, 3, 4, 0)
    orders = view_order.transpose(1, 0)
    image = None
    for view in range(VIEWS):
        shared = shared_spill(view, slices, phases)
        home, rim = render(view, phases, offsets, orders, density, emission)
        low = shifted(rim, "col", 1)
        high = low if lax.axis_size("col") == 2 else shifted(rim, "col", -1)
        canvas, up, down = fold(view, slices, length, phases, home, rim, low, high)
        above = shifted(down, "row", 1)
        below = shifted(up, "row", -1)
        kept, given = finish(view, shared, canvas, above, below)
        for level in range(levels - 1):
            kept, given = merge(view, level, orders, kept, swapped(given, level))
        image = emit(view, levels - 1, orders, kept, swapped(given, levels - 1), image)
    return image.reshape(VIEWS, 4, length // phases, 1, columns)


def solution(mesh):
    return jax.shard_map(
        local,
        mesh=mesh,
        in_specs=(
            P("depth", "row", "col"),
            P(None, "depth", "row", "col"),
            P(None, None, "depth", "row", "col"),
            P(None, "row"),
        ),
        out_specs=P(None, None, "row", "depth", "col"),
        check_vma=False,
    )
```

```python
import functools
import math
import jax
import jax.numpy as jnp
from jax import lax
from jax.experimental import pallas as pl
from jax.experimental.pallas import tpu as pltpu
from jax.sharding import PartitionSpec as P


MARGIN = 16
JIT = 8
VIEWS = 3

SHEAR_ROWS = (0.75, -0.5, 0.25)
SHEAR_COLS = (-0.25, 0.625, -0.875)

TILE = 8
GRID = 32
BF = jnp.bfloat16
F32 = jnp.float32
SMEM = pl.BlockSpec(memory_space=pltpu.SMEM)
VMEM = pl.BlockSpec(memory_space=pltpu.VMEM)
ANY = pl.BlockSpec(memory_space=pl.ANY)


def near(shape):
    return pltpu.VMEM(shape, F32)


def held(*arrays):
    return [pltpu.with_memory_space_constraint(array, pltpu.VMEM) for array in arrays]


def shared_spill(view, slices, phases):
    reach = abs(SHEAR_ROWS[view]) * (MARGIN - 2) * (slices - 1) / slices + JIT + 1
    need = -(-(math.ceil(reach) - 1) // phases)
    assert need <= TILE and phases & (phases - 1) == 0
    return 2 * need <= TILE


def canvas_rows(view, slices, phases, length):
    return length + (1 if shared_spill(view, slices, phases) else 2) * TILE * phases


def render_kernel(view, phases, offs, order, dens, emis, home, rim, turn, dbuf, ebuf, drow, dcol, hs, rs, sem):
    slices, length, columns = dens.shape
    bricks = columns // length
    half = length // 2
    quota = length // phases
    back = order[0, view] == 1
    turn[...] = jnp.full(turn.shape, order[0, view], jnp.int32)

    def slice_at(k):
        return jnp.where(back, slices - 1 - k, k)

    def copies(z):
        return (
            pltpu.make_async_copy(dens.at[z], dbuf.at[z], sem.at[0, z]),
            pltpu.make_async_copy(emis.at[:, z], ebuf.at[:, z], sem.at[1, z]),
        )

    for k in range(slices):
        for copy in copies(slice_at(k)):
            copy.start()

    def row_table(count, place):
        shape = (phases, count, length)
        phase = lax.broadcasted_iota(jnp.int32, shape, 0)
        spot = lax.broadcasted_iota(jnp.int32, shape, 1)
        source = lax.broadcasted_iota(jnp.int32, shape, 2)
        table = place(spot) * phases + phase - source
        return table.astype(F32).reshape(phases * count, length).astype(BF)

    spill = TILE * phases
    drow[0:length] = row_table(quota, lambda spot: spot)
    if drow.shape[0] == length + spill:
        drow[length:] = row_table(
            TILE, lambda spot: jnp.where(spot < TILE // 2, spot + quota, spot - TILE)
        )
    else:
        drow[length : length + spill] = row_table(TILE, lambda spot: spot - TILE)
        drow[length + spill :] = row_table(TILE, lambda spot: spot + quota)
    lane = lax.broadcasted_iota(jnp.int32, (length, length), 1)
    source = lax.broadcasted_iota(jnp.int32, (length, length), 0)
    dcol[0] = (lane - source).astype(F32).astype(BF)
    dcol[1] = (jnp.where(lane < half, lane + length, lane - length) - source).astype(F32).astype(BF)
    dcol[2] = (jnp.where(lane < half, lane - half, lane + half) - source).astype(F32).astype(BF)
    for ref in (home, rim):
        ref[0:3] = jnp.zeros((3,) + ref.shape[1:], F32)
        ref[3] = jnp.ones(ref.shape[1:], F32)

    def bilinear(distance, offset, rate, z):
        grid_rate = rate * (MARGIN - 2) * GRID / slices
        assert grid_rate == int(grid_rate)
        shift = offset * GRID + (2 * z - (slices - 1)) * int(grid_rate)
        whole = shift >> (GRID.bit_length() - 1)
        rest = (shift & (GRID - 1)).astype(F32) * (1.0 / GRID)
        near = (distance - whole.astype(F32).astype(BF)) - rest.astype(BF)
        one = jnp.ones((), BF)
        return jnp.maximum(one - jnp.abs(near), jnp.zeros((), BF))

    def resample(k, slot):
        z = slice_at(k)
        for copy in copies(z):
            copy.wait()
        for b in range(bricks):
            part = slice(b * length, (b + 1) * length)
            distance = jnp.concatenate([dcol[0], dcol[1 + b]], 1)
            weights = bilinear(distance, offs[1, 0, 0, b, view], SHEAR_COLS[view], z)
            cells = jnp.concatenate([dbuf[z, :, part]] + [ebuf[c, z, :, part] for c in range(3)], 0)
            resampled = jnp.dot(cells, weights, preferred_element_type=F32).astype(BF)
            for f in range(4):
                field = slice(f * length, (f + 1) * length)
                hs[slot, b, :, field] = resampled[field, :length]
                rs[slot, part, field] = resampled[field, length:]

    def shade(footprint, ref, part):
        through = ref[3, :, part]
        passed = through * jnp.exp(-footprint[:, :length])
        weight = through - passed
        ref[3, :, part] = passed
        for c in range(3):
            color = footprint[:, (c + 1) * length : (c + 2) * length]
            ref[c, :, part] = ref[c, :, part] + color * weight

    def deposit(k, slot):
        z = slice_at(k)
        weights = [
            bilinear(drow[...], offs[0, 0, 0, b, view], SHEAR_ROWS[view], z) for b in range(bricks)
        ]
        for b in range(bricks):
            shade(
                jnp.dot(weights[b], hs[slot, b], preferred_element_type=F32),
                home,
                slice(b * length, (b + 1) * length),
            )
        both = jnp.concatenate(weights, 1)
        shade(jnp.dot(both, rs[slot], preferred_element_type=F32), rim, slice(0, length))

    resample(0, 0)

    def step(pair, carry):
        k = 2 * pair
        resample(k + 1, 1)
        deposit(k, 0)
        resample(k + 2, 0)
        deposit(k + 1, 1)
        return carry

    assert slices % 2 == 0
    lax.fori_loop(0, slices // 2 - 1, step, 0)
    resample(slices - 1, 1)
    deposit(slices - 2, 0)
    deposit(slices - 1, 1)


def render(view, phases, offsets, orders, density, emission):
    slices, length, columns = density.shape
    rows = canvas_rows(view, slices, phases, length)
    bricks = columns // length
    assert bricks == 2 and length == 128
    return pl.pallas_call(
        functools.partial(render_kernel, view, phases),
        out_shape=(
            near((4, rows, columns)),
            near((4, rows, length)),
            pltpu.VMEM((TILE, 128), jnp.int32),
        ),
        in_specs=[SMEM, SMEM, ANY, ANY],
        out_specs=(VMEM,) * 3,
        scratch_shapes=[
            pltpu.VMEM(density.shape, BF),
            pltpu.VMEM(emission.shape, BF),
            pltpu.VMEM((rows, length), BF),
            pltpu.VMEM((3, length, length), BF),
            pltpu.VMEM((2, bricks, length, 4 * length), BF),
            pltpu.VMEM((2, bricks * length, 4 * length), BF),
            pltpu.SemaphoreType.DMA((2, slices)),
        ],
        compiler_params=pltpu.CompilerParams(vmem_limit_bytes=16 << 20),
    )(offsets, orders, density, emission)


def joined(channel, one, other):
    return one * other if channel == 3 else one + other


def fold_kernel(shared, phases, home, rim, low, high, canvas, up, down):
    columns = home.shape[2]
    lanes = columns // 2
    half, quarter = lanes // 2, lanes // 4
    quota = canvas.shape[2]
    length = quota * phases

    def folded(c, start, count):
        part = pl.ds(start, count)
        lane = lax.broadcasted_iota(jnp.int32, (count, lanes), 1)
        neutral = 1.0 if c == 3 else 0.0
        own = rim[c, part]
        first = jnp.where(lane < half, own, low[c, part])
        first = jnp.where((lane >= quarter) & (lane < lanes - quarter), first, neutral)
        second = jnp.where(lane < half, own, high[c, part])
        second = jnp.where((lane < quarter) | (lane >= lanes - quarter), second, neutral)
        return (
            joined(c, home[c, part, 0:lanes], pltpu.roll(first, half, 1)),
            joined(c, home[c, part, lanes:columns], second),
        )

    for c in range(4):
        for p in range(phases):
            one, other = folded(c, p * quota, quota)
            canvas[c, p, :, 0:lanes] = one
            canvas[c, p, :, lanes:columns] = other
        if shared:
            sub = lax.broadcasted_iota(jnp.int32, (TILE, lanes), 0)
            for j in range(phases // 2):
                one = folded(c, length + 2 * j * TILE, TILE)
                other = folded(c, length + (2 * j + 1) * TILE, TILE)
                for n in range(2):
                    turned = pltpu.roll(other[n], TILE // 2, 0)
                    part = slice(n * lanes, (n + 1) * lanes)
                    up[c, j, :, part] = jnp.where(sub < TILE // 2, turned, one[n])
                    down[c, j, :, part] = jnp.where(sub < TILE // 2, one[n], turned)
        else:
            for p in range(phases):
                for n, out in enumerate((up, down)):
                    one, other = folded(c, length + (n * phases + p) * TILE, TILE)
                    out[c, p, :, 0:lanes] = one
                    out[c, p, :, lanes:columns] = other


def fold(view, slices, length, phases, home, rim, low, high):
    columns = home.shape[2]
    shared = shared_spill(view, slices, phases)
    packs = phases // 2 if shared else phases
    return pl.pallas_call(
        functools.partial(fold_kernel, shared, phases),
        out_shape=(
            near((4, phases, length // phases, columns)),
            near((4, packs, TILE, columns)),
            near((4, packs, TILE, columns)),
        ),
        in_specs=[VMEM] * 4,
        out_specs=(VMEM,) * 3,
        compiler_params=pltpu.CompilerParams(vmem_limit_bytes=4 << 20),
    )(*held(home, rim, low, high))


def spills(shared, c, p, pack, odd, above, below):
    if not shared:
        return above[c, p], below[c, p]
    neutral = 1.0 if c == 3 else 0.0
    sub = lax.broadcasted_iota(jnp.int32, above.shape[2:], 0)
    top, bottom = above[c, pack], below[c, pack]
    top = jnp.where(odd == 1, pltpu.roll(top, TILE // 2, 0), top)
    bottom = jnp.where(odd == 1, pltpu.roll(bottom, TILE // 2, 0), bottom)
    return (
        jnp.where(sub < TILE // 2, top, neutral),
        jnp.where(sub < TILE // 2, neutral, bottom),
    )


def finish_kernel(shared, canvas, above, below, kept, given):
    bit = lax.axis_index("depth") & 1
    quota = canvas.shape[2]
    for n in range(kept.shape[1]):
        for out, odd in ((kept, bit), (given, 1 - bit)):
            p = 2 * n + odd
            for c in range(4):
                top, bottom = spills(shared, c, p, n, odd, above, below)
                out[c, n, 0:TILE] = joined(c, canvas[c, p, 0:TILE], top)
                if quota > 2 * TILE:
                    out[c, n, TILE : quota - TILE] = canvas[c, p, TILE : quota - TILE]
                out[c, n, quota - TILE :] = joined(c, canvas[c, p, quota - TILE :], bottom)


def finish(shared, canvas, above, below):
    channels, phases, quota, columns = canvas.shape
    return pl.pallas_call(
        functools.partial(finish_kernel, shared),
        out_shape=(near((channels, phases // 2, quota, columns)),) * 2,
        in_specs=[VMEM] * 3,
        out_specs=(VMEM,) * 2,
        compiler_params=pltpu.CompilerParams(vmem_limit_bytes=4 << 20),
    )(*held(canvas, above, below))


def over(ahead, own, other):
    front = [jnp.where(ahead, a, b) for a, b in zip(own, other)]
    rear = [jnp.where(ahead, b, a) for a, b in zip(own, other)]
    return [f + front[3] * r for f, r in zip(front[:3], rear[:3])] + [front[3] * rear[3]]


def own_ahead(level, turn, rows):
    me = lax.axis_index("depth")
    return jnp.broadcast_to(turn[0:1, :], (rows, turn.shape[1])) == (me >> level & 1)


def chunks(columns, lanes):
    return [slice(n, n + lanes) for n in range(0, columns, lanes)]


def merge_kernel(level, turn, kept, received, next_kept, next_given):
    quota, columns = kept.shape[2:]
    ahead = own_ahead(level, turn, quota)
    bit = lax.axis_index("depth") >> (level + 1) & 1
    for n in range(next_kept.shape[1]):
        for out, odd in ((next_kept, bit), (next_given, 1 - bit)):
            p = 2 * n + odd
            for part in chunks(columns, turn.shape[1]):
                own = [kept[c, p, :, part] for c in range(4)]
                other = [received[c, p, :, part] for c in range(4)]
                for c, pixels in enumerate(over(ahead, own, other)):
                    out[c, n, :, part] = pixels


def merge(level, turn, kept, received):
    channels, phases, quota, columns = kept.shape
    return pl.pallas_call(
        functools.partial(merge_kernel, level),
        out_shape=(near((channels, phases // 2, quota, columns)),) * 2,
        in_specs=[VMEM] * 3,
        out_specs=(VMEM,) * 2,
        compiler_params=pltpu.CompilerParams(vmem_limit_bytes=4 << 20),
    )(*held(turn, kept, received))


def emit_kernel(view, level, groups, turn, *refs):
    out, stage, sem = refs[-3:]
    lanes = stage.shape[2]
    start = 0
    for (indices, at, size) in groups:
        for n, part in enumerate(chunks(refs[indices[0]].shape[-1], lanes)):
            layers = [[refs[i][c, at : at + size, part] for c in range(4)] for i in indices]
            bit = level
            while len(layers) > 1:
                ahead = own_ahead(bit, turn, size)
                layers = [over(ahead, one, other) for one, other in zip(layers[0::2], layers[1::2])]
                bit += 1
            pieces = refs[indices[0]].shape[-1] // lanes
            for c in range(4):
                stage[c, pl.ds(start * pieces + n, size, stride=pieces), :] = layers[0][c]
        start += size
    copy = pltpu.make_async_copy(stage, out.at[view], sem)
    copy.start()
    copy.wait()


def emit(view, level, turn, blocks, groups, image):
    channels, _, columns = blocks[0].shape
    quota = sum(size for _, _, size in groups)
    shape = (channels, quota * columns // 128, 128)
    operands = held(turn, *blocks)
    specs = [VMEM] * len(operands)
    aliases = {}
    if image is not None:
        aliases = {len(operands): 0}
        operands.append(image)
        specs.append(ANY)
    return pl.pallas_call(
        functools.partial(emit_kernel, view, level, groups),
        out_shape=jax.ShapeDtypeStruct((VIEWS,) + shape, F32),
        in_specs=specs,
        out_specs=ANY,
        scratch_shapes=[pltpu.VMEM(shape, F32), pltpu.SemaphoreType.DMA],
        input_output_aliases=aliases,
        compiler_params=pltpu.CompilerParams(vmem_limit_bytes=4 << 20),
    )(*operands)


def inner_kernel(canvas, *outs):
    me = lax.axis_index("depth")
    for k, out in enumerate(outs):
        out[...] = canvas[:, me ^ k, TILE : TILE + out.shape[1]]


def split_inner(canvas):
    channels, phases, quota, columns = canvas.shape
    if quota == 2 * TILE:
        return []
    return pl.pallas_call(
        inner_kernel,
        out_shape=(near((channels, quota - 2 * TILE, columns)),) * phases,
        in_specs=[VMEM],
        out_specs=(VMEM,) * phases,
        compiler_params=pltpu.CompilerParams(vmem_limit_bytes=4 << 20),
    )(*held(canvas))


def edge_kernel(shared, canvas, above, below, *outs):
    me = lax.axis_index("depth")
    quota = canvas.shape[2]
    for k, out in enumerate(outs):
        p = me ^ k
        for c in range(4):
            top, bottom = spills(shared, c, p, p >> 1, p & 1, above, below)
            out[c, 0:TILE] = joined(c, canvas[c, p, 0:TILE], top)
            out[c, TILE:] = joined(c, canvas[c, p, quota - TILE :], bottom)


def split_edges(shared, canvas, above, below):
    channels, phases, _, columns = canvas.shape
    return pl.pallas_call(
        functools.partial(edge_kernel, shared),
        out_shape=(near((channels, 2 * TILE, columns)),) * phases,
        in_specs=[VMEM] * 3,
        out_specs=(VMEM,) * phases,
        compiler_params=pltpu.CompilerParams(vmem_limit_bytes=4 << 20),
    )(*held(canvas, above, below))


def shifted(block, axis, step):
    count = lax.axis_size(axis)
    return lax.ppermute(block, axis, [(i, (i + step) % count) for i in range(count)])


def swapped(block, flip):
    count = lax.axis_size("depth")
    return lax.ppermute(block, "depth", [(i, i ^ flip) for i in range(count)])


def canvas_of(view, density, emission, offsets, orders):
    slices, length = density.shape[:2]
    phases = lax.axis_size("depth")
    home, rim, turn = render(view, phases, offsets, orders, density, emission)
    low = shifted(rim, "col", 1)
    high = low if lax.axis_size("col") == 2 else shifted(rim, "col", -1)
    canvas, up, down = fold(view, slices, length, phases, home, rim, low, high)
    above = shifted(down, "row", 1)
    below = shifted(up, "row", -1)
    return canvas, above, below, turn


def local(density, emission, offsets, view_order):
    slices, length, columns = density.shape
    phases = lax.axis_size("depth")
    levels = phases.bit_length() - 1
    quota = length // phases
    offsets = offsets.transpose(1, 2, 3, 4, 0)
    orders = view_order.transpose(1, 0)
    density, emission, offsets, orders = (
        pltpu.with_memory_space_constraint(array, pltpu.HBM)
        for array in (density, emission, offsets, orders)
    )
    image = None
    for view in range(VIEWS):
        shared = shared_spill(view, slices, phases)
        canvas, above, below, turn = canvas_of(view, density, emission, offsets, orders)
        if view < VIEWS - 1:
            kept, given = finish(shared, canvas, above, below)
            for level in range(levels - 1):
                received = swapped(given, 1 << level)
                kept, given = merge(level, turn, kept, received)
            received = swapped(given, 1 << levels - 1)
            blocks = [kept[:, 0], received[:, 0]]
            groups = (((0, 1), 0, quota),)
            image = emit(view, levels - 1, turn, blocks, groups, image)
        else:
            inner = split_inner(canvas)
            inner = [swapped(b, k) if k else b for k, b in enumerate(inner)]
            edges = split_edges(shared, canvas, above, below)
            edges = [swapped(b, k) if k else b for k, b in enumerate(edges)]
            which = tuple(range(phases))
            groups = ((which, 0, TILE),)
            if inner:
                groups += ((tuple(phases + k for k in which), 0, quota - 2 * TILE),)
            groups += ((which, TILE, TILE),)
            image = emit(view, 0, turn, [*edges, *inner], groups, image)
    return image.reshape(VIEWS, 4, quota, 1, columns)


def solution(mesh):
    return jax.shard_map(
        local,
        mesh=mesh,
        in_specs=(
            P("depth", "row", "col"),
            P(None, "depth", "row", "col"),
            P(None, None, "depth", "row", "col"),
            P(None, "row"),
        ),
        out_specs=P(None, None, "row", "depth", "col"),
        check_vma=False,
    )
```
